32 devices in a mesh: parts: 2 (over x), seq: 16 (over z, y, core).
Axes of the slice: x: 2, y: 2, z: 4, core: 2. Of those that a mesh axis runs over, the one named last changes fastest.
Arguments:
- x_state: bfloat16 [32, 64, 384], P(('parts', 'seq')), parts along dimension 0, may hold values from -6 to 6
- noise_field: bfloat16 [32, 64, 384], P(('parts', 'seq')), parts along dimension 0, may hold values from -6 to 6
- rotations: float32 [9, 32, 64], P(None, ('parts', 'seq')), parts along dimension 1, may hold values from -1 to 1, as said below
- translations: float32 [3, 32, 64], P(None, ('parts', 'seq')), parts along dimension 1, may hold values from -15 to 15
- residue_types: int32 [128], P('parts'), parts along dimension 0, may hold values from 0 to 20
- pocket_mask: int32 [128], P('parts'), parts along dimension 0, may hold values 0 or 1
- type_table: bfloat16 [21, 384], replicated, may hold values from -3 to 3
- null_embed: bfloat16 [384], replicated, may hold values from -3 to 3
- spatial_gain: float32 [384], replicated, may hold values from 0.25 to 1.75
- spatial_proj: bfloat16 [384, 1152], replicated, may hold values from -0.3125 to 0.3125
- spatial_points: bfloat16 [384, 288], replicated, may hold values from -0.3125 to 0.3125
- spatial_gamma: float32 [12], replicated, may hold values from 0.2 to 2
- spatial_out: bfloat16 [384, 384], replicated, may hold values from -0.3125 to 0.3125
- temporal_gain: float32 [384], replicated, may hold values from 0.25 to 1.75
- temporal_proj: bfloat16 [384, 1152], replicated, may hold values from -0.3125 to 0.3125
- temporal_out: bfloat16 [384, 384], replicated, may hold values from -0.3125 to 0.3125
- hidden_gain: float32 [384], replicated, may hold values from 0.25 to 1.75
- hidden_in: bfloat16 [384, 1536], replicated, may hold values from -0.3125 to 0.3125
- hidden_out: bfloat16 [1536, 384], replicated, may hold values from -0.15625 to 0.15625
- head_gain: float32 [384], replicated, may hold values from 0.25 to 1.75
- head_out: bfloat16 [384, 384], replicated, may hold values from -0.3125 to 0.3125
Outputs:
- x_next: bfloat16 [32, 64, 384], P(('parts', 'seq')), parts along dimension 0
- velocity: bfloat16 [32, 64, 384], P(('parts', 'seq')), parts along dimension 0
The draws below stay inside these ranges and needn't reach their ends.
There are 2 independent parts, one for each index of `parts`. The reference program is written for one: setup_inputs(seed, part) draws one part's arguments, and reference() takes and returns one part's arrays. A program takes and returns all parts, laid end to end along the dimension named above; an argument that names none is the same for every part. Nothing has to cross between parts.
Inputs may be any that keep to these rules, and one draw needn't show every extreme that they name: `rotations`: each column over the first dimension is a proper rotation matrix, row-major.
All inputs are finite; a program needn't handle non-finite values.
Results may differ from the reference program's by a relative error of at most 0.015.
Values may be sent and summed in bfloat16 or wider, within the bound.
A program may use at most 64 MiB of HBM per device.

```python
import math
import jax
import jax.numpy as jnp
from jax import lax

WIDTH = 384
FEED_WIDTH = 1536
SHEADS = 12
THEADS = 6
POINTS = 4
TYPES = 21
FRAMES = 16
RESIDUES = 64


def draw_rotations(key, part):
    raw = jax.random.normal(key, (4, FRAMES, RESIDUES), jnp.float32)
    first = 1.0 + jnp.abs(raw[0])
    second = raw[1]
    third = raw[2]
    fourth = raw[3]
    length = jnp.sqrt(first * first + second * second + third * third + fourth * fourth)
    first = first / length
    second = second / length
    third = third / length
    fourth = fourth / length
    entries = [1.0 - 2.0 * (third * third + fourth * fourth), 2.0 * (second * third - first * fourth), 2.0 * (second * fourth + first * third), 2.0 * (second * third + first * fourth), 1.0 - 2.0 * (second * second + fourth * fourth), 2.0 * (third * fourth - first * second), 2.0 * (second * fourth - first * third), 2.0 * (third * fourth + first * second), 1.0 - 2.0 * (second * second + third * third)]
    return jnp.stack(entries)


def draw_translations(key, part):
    base = jax.random.normal(key, (3, FRAMES, RESIDUES), jnp.float32)
    values = 0.8 * base
    return jnp.clip(values, -15.0, 15.0)


def set_ends(values, key, smallest, largest):
    shape = values.shape
    place = [jax.random.randint(jax.random.fold_in(key, axis), (), 0, shape[axis]) for axis in range(len(shape))]
    values = values.at[tuple(place)].set(smallest)
    longest = shape.index(max(shape))
    place[longest] = (place[longest] + 1) % shape[longest]
    return values.at[tuple(place)].set(largest)


def block_levels(rng, shape, cuts, least, top_value):
    gain, own = 1.0, jax.random.fold_in(rng, 6)
    for dim, parts in cuts:
        heights = jnp.exp(jax.random.uniform(jax.random.fold_in(own, dim), (parts,), jnp.float32, least / len(cuts), top_value / len(cuts)))
        gain = gain * jnp.repeat(heights, shape[dim] // parts).reshape([-1 if axis == dim else 1 for axis in range(len(shape))])
    return gain


def noise(stream_key, shape, deviation, reach, shards=(), kind=jnp.bfloat16):
    array = jax.random.normal(stream_key, shape, jnp.float32) * deviation
    if len(shards) > 0:
        array = block_levels(stream_key, shape, shards, -0.22, 0.18) * array
    return jnp.clip(array, min=-reach, max=reach).astype(kind)


def setup_inputs(seed: int = 0, part: int = 0) -> dict:
    splits = jax.random.split(jax.random.key(seed), 22)
    part_splits = jax.random.split(jax.random.fold_in(splits[21], part), 22)
    return {
        "x_state": noise(part_splits[0], (FRAMES, RESIDUES, WIDTH), 1.0, 6.0, ((0, 16),)),
        "noise_field": noise(part_splits[1], (FRAMES, RESIDUES, WIDTH), 1.0, 6.0, ((0, 16),)),
        "rotations": draw_rotations(jax.random.fold_in(jax.random.fold_in(splits[21], part), 71), part),
        "translations": draw_translations(jax.random.fold_in(jax.random.fold_in(splits[21], part), 71), part),
        "residue_types": set_ends(jax.random.randint(part_splits[4], (RESIDUES,), 0, TYPES), jax.random.fold_in(part_splits[4], 1), 0, TYPES - 1).astype(jnp.int32),
        "pocket_mask": set_ends((jax.random.randint(part_splits[5], (RESIDUES,), 0, 4) < 3).astype(jnp.int32), jax.random.fold_in(part_splits[5], 1), 0, 1),
        "type_table": noise(splits[6], (TYPES, WIDTH), 0.5, 3.0),
        "null_embed": noise(splits[7], (WIDTH,), 0.5, 3.0),
        "spatial_gain": jnp.clip(1.0 + 0.15 * jax.random.normal(splits[8], (WIDTH,), jnp.float32), 0.25, 1.75),
        "spatial_proj": noise(splits[9], (WIDTH, 3 * WIDTH), WIDTH ** -0.5, 0.3125),
        "spatial_points": noise(splits[10], (WIDTH, 2 * SHEADS * POINTS * 3), WIDTH ** -0.5, 0.3125),
        "spatial_gamma": jnp.clip(jnp.exp(jax.random.uniform(splits[11], (SHEADS,), jnp.float32, math.log(0.2), math.log(2.0))), 0.2, 2.0),
        "spatial_out": noise(splits[12], (WIDTH, WIDTH), WIDTH ** -0.5, 0.3125),
        "temporal_gain": jnp.clip(1.0 + 0.15 * jax.random.normal(splits[13], (WIDTH,), jnp.float32), 0.25, 1.75),
        "temporal_proj": noise(splits[14], (WIDTH, 3 * WIDTH), WIDTH ** -0.5, 0.3125),
        "temporal_out": noise(splits[15], (WIDTH, WIDTH), WIDTH ** -0.5, 0.3125),
        "hidden_gain": jnp.clip(1.0 + 0.15 * jax.random.normal(splits[16], (WIDTH,), jnp.float32), 0.25, 1.75),
        "hidden_in": noise(splits[17], (WIDTH, FEED_WIDTH), WIDTH ** -0.5, 0.3125),
        "hidden_out": noise(splits[18], (FEED_WIDTH, WIDTH), FEED_WIDTH ** -0.5, 0.15625),
        "head_gain": jnp.clip(1.0 + 0.15 * jax.random.normal(splits[19], (WIDTH,), jnp.float32), 0.25, 1.75),
        "head_out": noise(splits[20], (WIDTH, WIDTH), WIDTH ** -0.5, 0.3125),
    }


WEIGHT_LOGIT = 0.7071067811865476
WEIGHT_POINT = 0.23570226039551584
GUIDE = 2.0
STEP_SIZE = 0.25
NOISE_SCALE = 0.2
EPSILON = 1e-05

def layer_norm(values, scale_gain):
    average = lax.optimization_barrier(jnp.mean(values, axis=-1, keepdims=True))
    centered = values - average
    spread = lax.optimization_barrier(jnp.mean(centered * centered, axis=-1, keepdims=True))
    return centered * lax.rsqrt(spread + EPSILON) * scale_gain

def softmax_rows(logits):
    row_max = lax.optimization_barrier(jnp.max(logits, axis=-1, keepdims=True))
    powers = jnp.exp(logits - row_max)
    return powers / lax.optimization_barrier(jnp.sum(powers, axis=-1, keepdims=True))

def branch_embed(residue_types, type_table, null_embed):
    count = type_table.shape[0]
    onehot = (residue_types[:, None] == jnp.arange(count, dtype=jnp.int32)[None, :]).astype(jnp.bfloat16)
    conditional = jnp.dot(onehot, type_table, preferred_element_type=jnp.float32)
    empty = jnp.broadcast_to(null_embed.astype(jnp.float32)[None, :], conditional.shape)
    return jnp.stack([conditional, empty])

def spatial_frame(state, rotation, translation, embedding, allowed, weights):
    spatial_gain, spatial_proj, spatial_points, spatial_gamma, spatial_out = weights
    branches, residues, model_width = embedding.shape
    head_count = spatial_gamma.shape[0]
    head_dim = model_width // head_count
    initial = state.astype(jnp.float32)[None] + embedding
    normed = layer_norm(initial, spatial_gain).astype(jnp.bfloat16).reshape(branches * residues, model_width)
    projected = jnp.dot(normed, spatial_proj, preferred_element_type=jnp.float32).astype(jnp.bfloat16)
    projected = projected.reshape(branches, residues, 3, head_count, head_dim).astype(jnp.float32)
    points = jnp.dot(normed, spatial_points, preferred_element_type=jnp.float32)
    points = points.reshape(branches, residues, 2, head_count, -1, 3)
    centred = translation - lax.optimization_barrier(jnp.mean(translation, axis=1, keepdims=True))
    turned = jnp.einsum('der,brshpe->bshpdr', rotation.reshape(3, 3, residues), points, precision=lax.Precision.HIGHEST)
    placed = turned + centred
    query_points = placed[:, 0].reshape(branches, head_count, -1, residues)
    key_points = placed[:, 1].reshape(branches, head_count, -1, residues)
    pairwise = jnp.einsum('bhcr,bhcs->bhrs', query_points, key_points, precision=lax.Precision.HIGHEST)
    query_norm = lax.optimization_barrier(jnp.sum(query_points * query_points, axis=2))
    key_norm = lax.optimization_barrier(jnp.sum(key_points * key_points, axis=2))
    distance = query_norm[..., :, None] + key_norm[..., None, :] - 2.0 * pairwise
    scalar = jnp.einsum('brhc,bshc->bhrs', projected[:, :, 0], projected[:, :, 1])
    logits = WEIGHT_LOGIT * scalar / jnp.sqrt(jnp.float32(head_dim)) - 0.5 * WEIGHT_LOGIT * WEIGHT_POINT * spatial_gamma[None, :, None, None] * distance
    logits = jnp.where(allowed[None, None], logits, -jnp.inf)
    attend = softmax_rows(logits).astype(jnp.bfloat16).astype(jnp.float32)
    context = jnp.einsum('bhrs,bshc->brhc', attend, projected[:, :, 2]).astype(jnp.bfloat16)
    update = jnp.dot(context.reshape(branches * residues, model_width), spatial_out, preferred_element_type=jnp.float32)
    return (initial + update.reshape(branches, residues, model_width)).astype(jnp.bfloat16)

def temporal_block(states, weights):
    temporal_gain, temporal_proj, temporal_out, hidden_gain, hidden_in, hidden_out = weights
    frames, branches, residues, model_width = states.shape
    head_dim = model_width // THEADS
    initial = states.astype(jnp.float32)
    normed = layer_norm(initial, temporal_gain).astype(jnp.bfloat16).reshape(-1, model_width)
    projected = jnp.dot(normed, temporal_proj, preferred_element_type=jnp.float32).astype(jnp.bfloat16)
    projected = projected.reshape(frames, branches, residues, 3, THEADS, head_dim).astype(jnp.float32)
    scores = jnp.einsum('qbrhc,kbrhc->brhqk', projected[:, :, :, 0], projected[:, :, :, 1]) / jnp.sqrt(jnp.float32(head_dim))
    attend = softmax_rows(scores).astype(jnp.bfloat16).astype(jnp.float32)
    context = jnp.einsum('brhqk,kbrhc->qbrhc', attend, projected[:, :, :, 2]).astype(jnp.bfloat16)
    after_time = initial + jnp.dot(context.reshape(-1, model_width), temporal_out, preferred_element_type=jnp.float32).reshape(states.shape)
    second = layer_norm(after_time, hidden_gain).astype(jnp.bfloat16).reshape(-1, model_width)
    feed_hidden = jax.nn.gelu(jnp.dot(second, hidden_in, preferred_element_type=jnp.float32)).astype(jnp.bfloat16)
    result = after_time + jnp.dot(feed_hidden, hidden_out, preferred_element_type=jnp.float32).reshape(states.shape)
    return result.astype(jnp.bfloat16)

def velocity_head(states, head_gain, head_out):
    model_width = states.shape[-1]
    normed = layer_norm(states.astype(jnp.float32), head_gain).astype(jnp.bfloat16).reshape(-1, model_width)
    branch_velocity = jnp.dot(normed, head_out, preferred_element_type=jnp.float32).reshape(states.shape)
    guided = branch_velocity[:, 1] + GUIDE * (branch_velocity[:, 0] - branch_velocity[:, 1])
    return guided.astype(jnp.bfloat16)

def reference(x_state, noise_field, rotations, translations, residue_types, pocket_mask, type_table, null_embed, spatial_gain, spatial_proj, spatial_points, spatial_gamma, spatial_out, temporal_gain, temporal_proj, temporal_out, hidden_gain, hidden_in, hidden_out, head_gain, head_out):
    embedding = branch_embed(residue_types, type_table, null_embed)
    residues = x_state.shape[1]
    allowed = (pocket_mask[None, :] == 1) | jnp.eye(residues, dtype=bool)
    spatial_weights = (spatial_gain, spatial_proj, spatial_points, spatial_gamma, spatial_out)
    time_weights = (temporal_gain, temporal_proj, temporal_out, hidden_gain, hidden_in, hidden_out)

    def one_frame(pieces):
        return spatial_frame(pieces[0], pieces[1], pieces[2], embedding, allowed, spatial_weights)
    spatial = lax.map(one_frame, (x_state, jnp.moveaxis(rotations, 1, 0), jnp.moveaxis(translations, 1, 0)))
    per_residue = jnp.moveaxis(spatial, 2, 0)

    def one_residue(column):
        return temporal_block(column[:, :, None, :], time_weights)[:, :, 0, :]
    mixed = jnp.moveaxis(lax.map(one_residue, per_residue), 0, 2)
    velocity = velocity_head(mixed, head_gain, head_out)
    x_next = (x_state.astype(jnp.float32) + STEP_SIZE * velocity.astype(jnp.float32) + NOISE_SCALE * noise_field.astype(jnp.float32)).astype(jnp.bfloat16)
    return (x_next, velocity)
```

```python
import functools

import jax
import jax.numpy as jnp
from jax import lax
from jax.experimental import pallas as pl
from jax.experimental.pallas import tpu as pltpu
from jax.sharding import PartitionSpec as P

THEADS = 6
WEIGHT_LOGIT = 0.7071067811865476
WEIGHT_POINT = 0.23570226039551584
GUIDE = 2.0
STEP_SIZE = 0.25
NOISE_SCALE = 0.2
EPSILON = 1e-05
BLOCK = 16
INPUTS = 20
VMEM_BYTES = 66_300_000
FINISH_BYTES = 1 << 20
GELU_SCALE = 0.7978845608028654

F32 = jnp.float32
BF16 = jnp.bfloat16
MESH = pl.DeviceIdType.MESH


def layer_norm(values, gain):
    average = jnp.mean(values, axis=-1, keepdims=True)
    centered = values - average
    spread = jnp.mean(centered * centered, axis=-1, keepdims=True)
    return centered * lax.rsqrt(spread + EPSILON) * gain


def dot(a, b):
    return jnp.dot(a, b, preferred_element_type=F32)


def dot_nt(a, b):
    return lax.dot_general(a, b, (((1,), (1,)), ((), ())), preferred_element_type=F32)


def dot_tn(a, b):
    return lax.dot_general(a, b, (((0,), (0,)), ((), ())), preferred_element_type=F32)


def iota(shape, axis):
    return lax.broadcasted_iota(jnp.int32, shape, axis)


def fold(values, op):
    rows = values.shape[0]
    while rows > 8:
        values = op(values[: rows // 2], values[rows // 2 :])
        rows //= 2
    return values


def softmax_down(logits):
    powers = jnp.exp(logits - jnp.max(fold(logits, jnp.maximum), axis=0, keepdims=True))
    return powers.astype(BF16), 1.0 / jnp.sum(fold(powers, jnp.add), axis=0, keepdims=True)


def interleave(first, second, share):
    rows, width = first.shape
    if 2 * share != 8:
        parts = [part.reshape(rows // share, share, width) for part in (first, second)]
        return jnp.concatenate(parts, axis=1)
    first, second = first.reshape(rows // 8, 8, width), second.reshape(rows // 8, 8, width)
    low = iota(first.shape, 1) < share
    even = jnp.where(low, first, pltpu.roll(second, share, 1))
    odd = jnp.where(low, pltpu.roll(first, share, 1), second)
    return jnp.stack([even, odd], axis=1).reshape(rows // share, 8, width)


def guide(both, share):
    n, group, width = both.shape
    if group != 8:
        return both[:, share:] + GUIDE * (both[:, :share] - both[:, share:])
    both = both.reshape(n // 2, 2, 8, width)
    even, odd = both[:, 0], both[:, 1]
    low = iota(even.shape, 1) < share
    first = jnp.where(low, even, pltpu.roll(odd, share, 1))
    second = jnp.where(low, pltpu.roll(even, share, 1), odd)
    return (second + GUIDE * (first - second)).reshape(n, share, width)


def split3(values):
    high = values.astype(BF16)
    rest = values - high.astype(F32)
    middle = rest.astype(BF16)
    low = (rest - middle.astype(F32)).astype(BF16)
    return high, middle, low


def kernel(n, *refs):
    sources, vel_ref, refs = refs[:INPUTS], refs[INPUTS], refs[INPUTS + 1 :]
    targets, refs = refs[:INPUTS], refs[INPUTS:]
    points, qfeat, kfeat, send1, recv1, send2, recv2, load_sem, s1, r1, s2, r2 = refs
    (x_ref, rot_ref, trans_ref, types_ref, mask_ref, table_ref, null_ref, sgain_ref, spts, sproj,
     gamma_ref, sout, tgain_ref, tproj, tout, hgain_ref, hin, hout, egain_ref, head) = targets
    me = lax.axis_index("seq")
    loads = [
        pltpu.make_async_copy(source, target, load_sem.at[index])
        for index, (source, target) in enumerate(zip(sources, targets))
    ]
    for load in loads:
        load.start()
    arrivals = iter(loads)

    def take(count):
        for _ in range(count):
            next(arrivals).wait()

    barrier = pltpu.get_barrier_semaphore()

    def greet(step, carry):
        pl.semaphore_signal(barrier, inc=1, device_id={"seq": lax.rem(me + step, n)}, device_id_type=MESH)
        return carry

    lax.fori_loop(1, n, greet, 0, unroll=True)

    _, residues, width = x_ref.shape
    share = residues // n
    group = 2 * share
    rows = 2 * residues
    sheads = gamma_ref.shape[0]
    head_dim = width // sheads
    npoints = spts.shape[0] // (6 * sheads)
    chunks = rows // points.shape[2]
    lanes = points.shape[2]

    take(8)
    trans = trans_ref[...].reshape(3, residues)
    trans = trans - jnp.mean(trans, axis=1, keepdims=True)
    frames = jnp.concatenate([rot_ref[...].reshape(9, residues), trans], axis=0)
    frames = jnp.concatenate([frames, frames], axis=1)

    kinds = table_ref.shape[0]
    types_row = types_ref[...].astype(F32).reshape(1, residues)
    onehot = (iota((kinds, residues), 0).astype(F32) == types_row).astype(BF16)
    x_rows = x_ref[0].astype(F32)
    initial = jnp.concatenate(
        [x_rows + dot_tn(onehot, table_ref[...]), x_rows + null_ref[...].astype(F32).reshape(1, width)], axis=0
    )
    normed = layer_norm(initial, sgain_ref[...].reshape(1, width)).astype(BF16)

    j_ids = iota((residues, residues), 0)
    i_ids = iota((residues, residues), 1)
    mask_row = mask_ref[...].astype(F32).reshape(1, residues)
    mask_col = jnp.sum(jnp.where(j_ids == i_ids, mask_row, 0.0), axis=1, keepdims=True)
    bias = jnp.where((mask_col == 1.0) | (j_ids == i_ids), 0.0, -jnp.inf)
    bias = jnp.concatenate([bias, bias], axis=1)
    left = iota((residues, rows), 1) < residues

    take(1)
    pts = dot_nt(spts[...], normed)
    for c in range(chunks):
        points[c] = pts[:, c * lanes : (c + 1) * lanes]
    take(1)
    projected = dot(normed, sproj[...]).astype(BF16)
    turned = projected.T
    q_t = turned[:width] * BF16(WEIGHT_LOGIT / head_dim**0.5)
    k_t = turned[width : 2 * width]
    v_t = turned[2 * width :]

    take(1)
    eye = iota((sheads, sheads), 0) == iota((sheads, sheads), 1)
    gamma_col = jnp.sum(jnp.where(eye, gamma_ref[...].reshape(1, sheads), 0.0), axis=1, keepdims=True)
    weight_col = (WEIGHT_LOGIT * WEIGHT_POINT) * gamma_col
    ones = jnp.ones((sheads, lanes), F32)
    qfeat[...] = jnp.zeros_like(qfeat)
    kfeat[...] = jnp.zeros_like(kfeat)
    for c in range(chunks):
        frame = frames[:, c * lanes : (c + 1) * lanes]
        for side, feat in ((0, qfeat), (1, kfeat)):
            norm = jnp.zeros((sheads, lanes), F32)
            for p in range(npoints):
                local = [
                    points[c, pl.ds(side * sheads * npoints * 3 + p * 3 + e, sheads, stride=npoints * 3), :]
                    for e in range(3)
                ]
                for d in range(3):
                    placed = (
                        frame[3 * d : 3 * d + 1] * local[0]
                        + frame[3 * d + 1 : 3 * d + 2] * local[1]
                        + frame[3 * d + 2 : 3 * d + 3] * local[2]
                        + frame[9 + d : 10 + d]
                    )
                    norm = norm + placed * placed
                    feat[c, pl.ds(d * npoints + p, sheads, stride=BLOCK), :] = (
                        placed * weight_col if side == 0 else placed
                    )
            norm = norm * (-0.5 * weight_col)
            last = 3 * npoints
            feat[c, pl.ds(last, sheads, stride=BLOCK), :] = norm if side == 0 else ones
            feat[c, pl.ds(last + 1, sheads, stride=BLOCK), :] = ones if side == 0 else norm

    q_parts = split3(jnp.concatenate([qfeat[c] for c in range(chunks)], axis=1))
    k_parts = split3(jnp.concatenate([kfeat[c] for c in range(chunks)], axis=1))
    contexts = []
    for h in range(sheads):
        scalar = slice(h * head_dim, (h + 1) * head_dim)
        block = slice(h * BLOCK, (h + 1) * BLOCK)
        q_h = jnp.concatenate([q_t[scalar]] + [q_parts[t][block] for t in (0, 0, 1, 0, 2, 1)], axis=0)
        k_h = jnp.concatenate([k_t[scalar]] + [k_parts[t][block] for t in (0, 1, 0, 2, 0, 1)], axis=0)
        v_h = v_t[scalar]
        if residues % 128:
            scores = dot_tn(k_h, q_h)
            attend, inverse = softmax_down(jnp.where(left, scores[:residues], scores[residues:]) + bias)
            blank = jnp.zeros_like(attend)
            attend = jnp.concatenate([jnp.where(left, attend, blank), jnp.where(left, blank, attend)], axis=0)
            contexts.append((dot(v_h, attend) * inverse).astype(BF16))
        else:
            halves = [slice(b * residues, (b + 1) * residues) for b in range(2)]
            scores = jnp.concatenate([dot_tn(k_h[:, half], q_h[:, half]) for half in halves], axis=1)
            attend, inverse = softmax_down(scores + bias)
            mixed = jnp.concatenate([dot(v_h[:, half], attend[:, half]) for half in halves], axis=1)
            contexts.append((mixed * inverse).astype(BF16))
    context = jnp.concatenate(contexts, axis=0).T
    take(1)
    state = initial + dot(context, sout[...])
    send1[...] = interleave(state[:residues], state[residues:], share).astype(BF16)

    pl.semaphore_wait(barrier, n - 1)

    bits = [lax.rem(me // 2**k, 2) for k in range((n - 1).bit_length())]

    def partner(step):
        return me + sum((1 - 2 * bit) * 2**k for k, bit in enumerate(bits) if (step >> k) & 1)

    def swap(source, target, send_sem, recv_sem):
        for step in range(n - 1, 0, -1):
            other = partner(step)
            pltpu.make_async_remote_copy(
                src_ref=source.at[other], dst_ref=target.at[me], send_sem=send_sem,
                recv_sem=recv_sem, device_id={"seq": other}, device_id_type=MESH,
            ).start()
        target[me] = source[me]
        pltpu.make_async_copy(target.at[pl.ds(0, n - 1)], target.at[pl.ds(0, n - 1)], recv_sem).wait()

    swap(send1, recv1, s1, r1)
    take(8)

    count = n * group
    state = recv1[...].astype(F32).reshape(count, width)
    normed = layer_norm(state, tgain_ref[...].reshape(1, width)).astype(BF16)
    projected = dot(normed, tproj[...]).astype(BF16)
    same = (iota((count, count), 0) & (group - 1)) == (iota((count, count), 1) & (group - 1))
    bias = jnp.where(same, 0.0, -jnp.inf)
    tdim = width // THEADS
    pair = 128 // tdim
    lane_head = iota((1, 128), 1) >> (tdim.bit_length() - 1)
    v_t = projected[:, 2 * width :].T
    logits = []
    for g in range(width // 128):
        q_g = projected[:, g * 128 : (g + 1) * 128] * BF16(tdim**-0.5)
        k_g = projected[:, width + g * 128 : width + (g + 1) * 128]
        q_g = jnp.concatenate([jnp.where(lane_head == part, q_g, BF16(0.0)) for part in range(pair)], axis=0)
        scores = dot_nt(k_g, q_g)
        logits += [scores[:, part * count : (part + 1) * count] + bias for part in range(pair)]
    attends = [softmax_down(part) for part in logits]
    contexts = [
        (dot(v_t[h * tdim : (h + 1) * tdim], attend) * inverse).astype(BF16)
        for h, (attend, inverse) in enumerate(attends)
    ]
    context = jnp.concatenate(contexts, axis=0).T
    after = state + dot(context, tout[...])
    second = layer_norm(after, hgain_ref[...].reshape(1, width)).astype(BF16)
    hidden = dot(second, hin[...])
    inner = hidden * (GELU_SCALE + (GELU_SCALE * 0.044715) * (hidden * hidden))
    doubled = (hidden + hidden * jnp.tanh(inner)).astype(BF16)
    mixed = (after + 0.5 * dot(doubled, hout[...])).astype(BF16).astype(F32)
    normed = layer_norm(mixed, egain_ref[...].reshape(1, width)).astype(BF16)
    both = dot(normed, head[...]).reshape(n, group, width)
    send2[...] = guide(both, share).astype(BF16)
    swap(send2, recv2, s2, r2)
    vel_ref[...] = recv2[...].astype(F32).reshape(residues, width).astype(BF16)
    for source, sem in ((send1, s1), (send2, s2)):
        pltpu.make_async_copy(source.at[pl.ds(0, n - 1)], source.at[pl.ds(0, n - 1)], sem).wait()


def finish_kernel(raw_ref, x_ref, noise_ref, next_ref, vel_ref):
    velocity = raw_ref[...]
    vel_ref[0] = velocity
    next_ref[0] = (
        x_ref[0].astype(F32) + STEP_SIZE * velocity.astype(F32) + NOISE_SCALE * noise_ref[0].astype(F32)
    ).astype(BF16)


def body(n, x_state, noise_field, rotations, translations, residue_types, pocket_mask, type_table,
         null_embed, spatial_gain, spatial_proj, spatial_points, spatial_gamma, spatial_out,
         temporal_gain, temporal_proj, temporal_out, hidden_gain, hidden_in, hidden_out,
         head_gain, head_out):
    _, residues, width = x_state.shape
    share = residues // n
    rows = 2 * residues
    sheads = spatial_gamma.shape[0]
    chunks = rows // 128
    inputs = [x_state, rotations, translations, residue_types, pocket_mask, type_table, null_embed,
              spatial_gain, spatial_points.T, spatial_proj, spatial_gamma, spatial_out,
              temporal_gain, temporal_proj, temporal_out, hidden_gain, hidden_in, hidden_out,
              head_gain, head_out]
    dma = pltpu.SemaphoreType.DMA
    velocity = pl.pallas_call(
        functools.partial(kernel, n),
        out_shape=pltpu.VMEM((residues, width), BF16),
        in_specs=[pl.BlockSpec(memory_space=pltpu.HBM)] * INPUTS,
        out_specs=pl.BlockSpec(memory_space=pltpu.VMEM),
        scratch_shapes=[pltpu.VMEM(w.shape, w.dtype) for w in inputs]
        + [
            pltpu.VMEM((chunks, spatial_points.shape[1], 128), F32),
            pltpu.VMEM((chunks, sheads * BLOCK, 128), F32),
            pltpu.VMEM((chunks, sheads * BLOCK, 128), F32),
            pltpu.VMEM((n, 2 * share, width), BF16),
            pltpu.VMEM((n, 2 * share, width), BF16),
            pltpu.VMEM((n, share, width), BF16),
            pltpu.VMEM((n, share, width), BF16),
            dma((INPUTS,)), dma, dma, dma, dma,
        ],
        compiler_params=pltpu.CompilerParams(
            collective_id=0, has_side_effects=True, vmem_limit_bytes=VMEM_BYTES
        ),
    )(*inputs)
    whole = pl.BlockSpec(memory_space=pltpu.VMEM)
    return pl.pallas_call(
        finish_kernel,
        out_shape=(jax.ShapeDtypeStruct(x_state.shape, BF16),) * 2,
        in_specs=[whole] * 3,
        out_specs=(whole, whole),
        compiler_params=pltpu.CompilerParams(vmem_limit_bytes=FINISH_BYTES),
    )(velocity, x_state, noise_field)


def solution(mesh):
    split = P(("parts", "seq"), None, None)
    frames = P(None, ("parts", "seq"), None)
    return jax.shard_map(
        functools.partial(body, mesh.shape["seq"]),
        mesh=mesh,
        in_specs=(split, split, frames, frames, P("parts"), P("parts")) + (P(),) * 15,
        out_specs=(split, split),
        check_vma=False,
    )
```

```python
import functools

import jax
import jax.numpy as jnp
from jax import lax
from jax.experimental import pallas as pl
from jax.experimental.pallas import tpu as pltpu
from jax.sharding import PartitionSpec as P

THEADS = 6
WEIGHT_LOGIT = 0.7071067811865476
WEIGHT_POINT = 0.23570226039551584
GUIDE = 2.0
STEP_SIZE = 0.25
NOISE_SCALE = 0.2
EPSILON = 1e-05
BLOCK = 16
INPUTS = 20
VMEM_BYTES = 66_300_000
FINISH_BYTES = 1 << 20
GELU_SCALE = 0.7978845608028654

F32 = jnp.float32
BF16 = jnp.bfloat16
MESH = pl.DeviceIdType.MESH


def layer_norm(values, gain):
    average = jnp.mean(values, axis=-1, keepdims=True)
    centered = values - average
    spread = jnp.mean(centered * centered, axis=-1, keepdims=True)
    return centered * lax.rsqrt(spread + EPSILON) * gain


def dot(a, b):
    return jnp.dot(a, b, preferred_element_type=F32)


def dot_nt(a, b):
    return lax.dot_general(a, b, (((1,), (1,)), ((), ())), preferred_element_type=F32)


def dot_tn(a, b):
    return lax.dot_general(a, b, (((0,), (0,)), ((), ())), preferred_element_type=F32)


def iota(shape, axis):
    return lax.broadcasted_iota(jnp.int32, shape, axis)


def fold(values, op):
    rows = values.shape[0]
    while rows > 8:
        values = op(values[: rows // 2], values[rows // 2 :])
        rows //= 2
    return values


def softmax_down(logits):
    powers = jnp.exp(logits - jnp.max(fold(logits, jnp.maximum), axis=0, keepdims=True))
    return powers.astype(BF16), 1.0 / jnp.sum(fold(powers, jnp.add), axis=0, keepdims=True)


def interleave(first, second, share):
    rows, width = first.shape
    if 2 * share != 8:
        parts = [part.reshape(rows // share, share, width) for part in (first, second)]
        return jnp.concatenate(parts, axis=1)
    first, second = first.reshape(rows // 8, 8, width), second.reshape(rows // 8, 8, width)
    low = iota(first.shape, 1) < share
    even = jnp.where(low, first, pltpu.roll(second, share, 1))
    odd = jnp.where(low, pltpu.roll(first, share, 1), second)
    return jnp.stack([even, odd], axis=1).reshape(rows // share, 8, width)


def guide(both, share):
    n, group, width = both.shape
    if group != 8:
        return both[:, share:] + GUIDE * (both[:, :share] - both[:, share:])
    both = both.reshape(n // 2, 2, 8, width)
    even, odd = both[:, 0], both[:, 1]
    low = iota(even.shape, 1) < share
    first = jnp.where(low, even, pltpu.roll(odd, share, 1))
    second = jnp.where(low, pltpu.roll(even, share, 1), odd)
    return (second + GUIDE * (first - second)).reshape(n, share, width)


def split3(values):
    high = values.astype(BF16)
    rest = values - high.astype(F32)
    middle = rest.astype(BF16)
    low = (rest - middle.astype(F32)).astype(BF16)
    return high, middle, low


def kernel(n, *refs):
    sources, vel_ref, refs = refs[:INPUTS], refs[INPUTS], refs[INPUTS + 1 :]
    targets, refs = refs[:INPUTS], refs[INPUTS:]
    points, qfeat, kfeat, send1, recv1, send2, recv2, saved, load_sem, s1, r1, s2, r2 = refs
    (x_ref, rot_ref, trans_ref, types_ref, mask_ref, table_ref, null_ref, sgain_ref, spts, sproj,
     gamma_ref, sout, tgain_ref, tproj, tout, hgain_ref, hin, hout, egain_ref, head) = targets
    me = lax.axis_index("seq")
    loads = [
        pltpu.make_async_copy(source, target, load_sem.at[index])
        for index, (source, target) in enumerate(zip(sources, targets))
    ]
    for load in loads:
        load.start()
    arrivals = iter(loads)

    def take(count):
        for _ in range(count):
            next(arrivals).wait()

    barrier = pltpu.get_barrier_semaphore()

    def greet(step, carry):
        pl.semaphore_signal(barrier, inc=1, device_id={"seq": lax.rem(me + step, n)}, device_id_type=MESH)
        return carry

    lax.fori_loop(1, n, greet, 0, unroll=True)

    _, residues, width = x_ref.shape
    share = residues // n
    group = 2 * share
    rows = 2 * residues
    sheads = gamma_ref.shape[0]
    head_dim = width // sheads
    npoints = spts.shape[0] // (6 * sheads)
    chunks = rows // points.shape[2]
    lanes = points.shape[2]

    take(8)
    trans = trans_ref[...].reshape(3, residues)
    trans = trans - jnp.mean(trans, axis=1, keepdims=True)
    frames = jnp.concatenate([rot_ref[...].reshape(9, residues), trans], axis=0)
    frames = jnp.concatenate([frames, frames], axis=1)

    kinds = table_ref.shape[0]
    types_row = types_ref[...].astype(F32).reshape(1, residues)
    onehot = (iota((kinds, residues), 0).astype(F32) == types_row).astype(BF16)
    x_rows = x_ref[0].astype(F32)
    initial = jnp.concatenate(
        [x_rows + dot_tn(onehot, table_ref[...]), x_rows + null_ref[...].astype(F32).reshape(1, width)], axis=0
    )
    normed = layer_norm(initial, sgain_ref[...].reshape(1, width)).astype(BF16)

    j_ids = iota((residues, residues), 0)
    i_ids = iota((residues, residues), 1)
    mask_row = mask_ref[...].astype(F32).reshape(1, residues)
    mask_col = jnp.sum(jnp.where(j_ids == i_ids, mask_row, 0.0), axis=1, keepdims=True)
    bias = jnp.where((mask_col == 1.0) | (j_ids == i_ids), 0.0, -jnp.inf)
    bias = jnp.concatenate([bias, bias], axis=1)
    left = iota((residues, rows), 1) < residues

    take(1)
    pts = dot_nt(spts[...], normed)
    for c in range(chunks):
        points[c] = pts[:, c * lanes : (c + 1) * lanes]
    take(1)
    projected = dot(normed, sproj[...]).astype(BF16)
    turned = projected.T
    q_t = turned[:width] * BF16(WEIGHT_LOGIT / head_dim**0.5)
    k_t = turned[width : 2 * width]
    v_t = turned[2 * width :]

    take(1)
    eye = iota((sheads, sheads), 0) == iota((sheads, sheads), 1)
    gamma_col = jnp.sum(jnp.where(eye, gamma_ref[...].reshape(1, sheads), 0.0), axis=1, keepdims=True)
    weight_col = (WEIGHT_LOGIT * WEIGHT_POINT) * gamma_col
    ones = jnp.ones((sheads, lanes), F32)
    qfeat[...] = jnp.zeros_like(qfeat)
    kfeat[...] = jnp.zeros_like(kfeat)
    for c in range(chunks):
        frame = frames[:, c * lanes : (c + 1) * lanes]
        for side, feat in ((0, qfeat), (1, kfeat)):
            norm = jnp.zeros((sheads, lanes), F32)
            for p in range(npoints):
                local = [
                    points[c, pl.ds(side * sheads * npoints * 3 + p * 3 + e, sheads, stride=npoints * 3), :]
                    for e in range(3)
                ]
                for d in range(3):
                    placed = (
                        frame[3 * d : 3 * d + 1] * local[0]
                        + frame[3 * d + 1 : 3 * d + 2] * local[1]
                        + frame[3 * d + 2 : 3 * d + 3] * local[2]
                        + frame[9 + d : 10 + d]
                    )
                    norm = norm + placed * placed
                    feat[c, pl.ds(d * npoints + p, sheads, stride=BLOCK), :] = (
                        placed * weight_col if side == 0 else placed
                    )
            norm = norm * (-0.5 * weight_col)
            last = 3 * npoints
            feat[c, pl.ds(last, sheads, stride=BLOCK), :] = norm if side == 0 else ones
            feat[c, pl.ds(last + 1, sheads, stride=BLOCK), :] = ones if side == 0 else norm

    q_parts = split3(jnp.concatenate([qfeat[c] for c in range(chunks)], axis=1))
    k_parts = split3(jnp.concatenate([kfeat[c] for c in range(chunks)], axis=1))
    contexts = []
    for h in range(sheads):
        scalar = slice(h * head_dim, (h + 1) * head_dim)
        block = slice(h * BLOCK, (h + 1) * BLOCK)
        q_h = jnp.concatenate([q_t[scalar]] + [q_parts[t][block] for t in (0, 0, 1, 0, 2, 1)], axis=0)
        k_h = jnp.concatenate([k_t[scalar]] + [k_parts[t][block] for t in (0, 1, 0, 2, 0, 1)], axis=0)
        v_h = v_t[scalar]
        if residues % 128:
            scores = dot_tn(k_h, q_h)
            attend, inverse = softmax_down(jnp.where(left, scores[:residues], scores[residues:]) + bias)
            blank = jnp.zeros_like(attend)
            attend = jnp.concatenate([jnp.where(left, attend, blank), jnp.where(left, blank, attend)], axis=0)
            contexts.append((dot(v_h, attend) * inverse).astype(BF16))
        else:
            halves = [slice(b * residues, (b + 1) * residues) for b in range(2)]
            scores = jnp.concatenate([dot_tn(k_h[:, half], q_h[:, half]) for half in halves], axis=1)
            attend, inverse = softmax_down(scores + bias)
            mixed = jnp.concatenate([dot(v_h[:, half], attend[:, half]) for half in halves], axis=1)
            contexts.append((mixed * inverse).astype(BF16))
    context = jnp.concatenate(contexts, axis=0).T
    take(1)
    state = initial + dot(context, sout[...])
    send1[...] = interleave(state[:residues], state[residues:], share).astype(BF16)

    pl.semaphore_wait(barrier, n - 1)

    bits = [lax.rem(me // 2**k, 2) for k in range((n - 1).bit_length())]

    def partner(step):
        return me + sum((1 - 2 * bit) * 2**k for k, bit in enumerate(bits) if (step >> k) & 1)

    def swap(source, target, send_sem, recv_sem):
        for step in range(n - 1, 0, -1):
            other = partner(step)
            pltpu.make_async_remote_copy(
                src_ref=source.at[other], dst_ref=target.at[me], send_sem=send_sem,
                recv_sem=recv_sem, device_id={"seq": other}, device_id_type=MESH,
            ).start()
        target[me] = source[me]
        pltpu.make_async_copy(target.at[pl.ds(0, n - 1)], target.at[pl.ds(0, n - 1)], recv_sem).wait()

    swap(send1, recv1, s1, r1)
    take(8)

    count = n * group
    state = recv1[...].astype(F32).reshape(count, width)
    normed = layer_norm(state, tgain_ref[...].reshape(1, width)).astype(BF16)
    projected = dot(normed, tproj[...]).astype(BF16)
    same = (iota((count, count), 0) & (group - 1)) == (iota((count, count), 1) & (group - 1))
    bias = jnp.where(same, 0.0, -jnp.inf)
    tdim = width // THEADS
    pair = 128 // tdim
    lane_head = iota((1, 128), 1) >> (tdim.bit_length() - 1)
    v_t = projected[:, 2 * width :].T
    logits = []
    for g in range(width // 128):
        q_g = projected[:, g * 128 : (g + 1) * 128] * BF16(tdim**-0.5)
        k_g = projected[:, width + g * 128 : width + (g + 1) * 128]
        q_g = jnp.concatenate([jnp.where(lane_head == part, q_g, BF16(0.0)) for part in range(pair)], axis=0)
        scores = dot_nt(k_g, q_g)
        logits += [scores[:, part * count : (part + 1) * count] + bias for part in range(pair)]
    attends = [softmax_down(part) for part in logits]
    contexts = [
        (dot(v_t[h * tdim : (h + 1) * tdim], attend) * inverse).astype(BF16)
        for h, (attend, inverse) in enumerate(attends)
    ]
    context = jnp.concatenate(contexts, axis=0).T
    saved[...] = context

    def finish_rows(first, last):
        frames_in = slice(first // group, last // group)
        state = recv1[frames_in].astype(F32).reshape(last - first, width)
        after = state + dot(saved[first:last], tout[...])
        second = layer_norm(after, hgain_ref[...].reshape(1, width)).astype(BF16)
        hidden = dot(second, hin[...])
        inner = hidden * (GELU_SCALE + (GELU_SCALE * 0.044715) * (hidden * hidden))
        doubled = (hidden + hidden * jnp.tanh(inner)).astype(BF16)
        mixed = (after + 0.5 * dot(doubled, hout[...])).astype(BF16).astype(F32)
        normed = layer_norm(mixed, egain_ref[...].reshape(1, width)).astype(BF16)
        both = dot(normed, head[...]).reshape((last - first) // group, group, width)
        send2[frames_in] = guide(both, share).astype(BF16)

    def reply(device):
        pltpu.make_async_remote_copy(
            src_ref=send2.at[device], dst_ref=recv2.at[me], send_sem=s2,
            recv_sem=r2, device_id={"seq": device}, device_id_type=MESH,
        ).start()

    finish_rows(0, 2 * group)
    for device in range(2):
        pl.when(me != device)(functools.partial(reply, device))

    @pl.when(me < n)
    def _():
        finish_rows(2 * group, count)

    for step in range(2, n - 1):
        reply(step + ((me >= 2) & (step >= me)).astype(jnp.int32))
    pl.when(me < 2)(functools.partial(reply, n - 1))
    recv2[me] = send2[me]
    pltpu.make_async_copy(recv2.at[pl.ds(0, n - 1)], recv2.at[pl.ds(0, n - 1)], r2).wait()
    vel_ref[...] = recv2[...].astype(F32).reshape(residues, width).astype(BF16)
    for source, sem in ((send1, s1), (send2, s2)):
        pltpu.make_async_copy(source.at[pl.ds(0, n - 1)], source.at[pl.ds(0, n - 1)], sem).wait()


def finish_kernel(raw_ref, x_ref, noise_ref, next_ref, vel_ref):
    velocity = raw_ref[...]
    vel_ref[0] = velocity
    next_ref[0] = (
        x_ref[0].astype(F32) + STEP_SIZE * velocity.astype(F32) + NOISE_SCALE * noise_ref[0].astype(F32)
    ).astype(BF16)


def body(n, x_state, noise_field, rotations, translations, residue_types, pocket_mask, type_table,
         null_embed, spatial_gain, spatial_proj, spatial_points, spatial_gamma, spatial_out,
         temporal_gain, temporal_proj, temporal_out, hidden_gain, hidden_in, hidden_out,
         head_gain, head_out):
    _, residues, width = x_state.shape
    share = residues // n
    rows = 2 * residues
    sheads = spatial_gamma.shape[0]
    chunks = rows // 128
    inputs = [x_state, rotations, translations, residue_types, pocket_mask, type_table, null_embed,
              spatial_gain, spatial_points.T, spatial_proj, spatial_gamma, spatial_out,
              temporal_gain, temporal_proj, temporal_out, hidden_gain, hidden_in, hidden_out,
              head_gain, head_out]
    dma = pltpu.SemaphoreType.DMA
    velocity = pl.pallas_call(
        functools.partial(kernel, n),
        out_shape=pltpu.VMEM((residues, width), BF16),
        in_specs=[pl.BlockSpec(memory_space=pltpu.HBM)] * INPUTS,
        out_specs=pl.BlockSpec(memory_space=pltpu.VMEM),
        scratch_shapes=[pltpu.VMEM(w.shape, w.dtype) for w in inputs]
        + [
            pltpu.VMEM((chunks, spatial_points.shape[1], 128), F32),
            pltpu.VMEM((chunks, sheads * BLOCK, 128), F32),
            pltpu.VMEM((chunks, sheads * BLOCK, 128), F32),
            pltpu.VMEM((n, 2 * share, width), BF16),
            pltpu.VMEM((n, 2 * share, width), BF16),
            pltpu.VMEM((n, share, width), BF16),
            pltpu.VMEM((n, share, width), BF16),
            pltpu.VMEM((2 * residues, width), BF16),
            dma((INPUTS,)), dma, dma, dma, dma,
        ],
        compiler_params=pltpu.CompilerParams(
            collective_id=0, has_side_effects=True, vmem_limit_bytes=VMEM_BYTES
        ),
    )(*inputs)
    whole = pl.BlockSpec(memory_space=pltpu.VMEM)
    return pl.pallas_call(
        finish_kernel,
        out_shape=(jax.ShapeDtypeStruct(x_state.shape, BF16),) * 2,
        in_specs=[whole] * 3,
        out_specs=(whole, whole),
        compiler_params=pltpu.CompilerParams(vmem_limit_bytes=FINISH_BYTES),
    )(velocity, x_state, noise_field)


def solution(mesh):
    split = P(("parts", "seq"), None, None)
    frames = P(None, ("parts", "seq"), None)
    return jax.shard_map(
        functools.partial(body, mesh.shape["seq"]),
        mesh=mesh,
        in_specs=(split, split, frames, frames, P("parts"), P("parts")) + (P(),) * 15,
        out_specs=(split, split),
        check_vma=False,
    )
```
